32 devices in a mesh: tm: 4 (over z), tmpl: 8 (over y, x, core).
Axes of the slice: x: 2, y: 2, z: 4, core: 2. Of those that a mesh axis runs over, the one named last changes fastest.
Arguments:
- strain: float32 [8, 131072], P('tmpl', 'tm'), may hold values from -6 to 6
- psd_bins: int32 [4, 65536], P(None, 'tmpl'), may hold values from 0 to 8191, as said below
- psd_values: float32 [4, 8192], P('tm'), may hold values from 0.25 to 4
- chirp_slope: int32 [16], P('tmpl'), may hold values from 0 to 1023
- chirp_curve: int32 [16], P('tmpl'), may hold values from 1 to 63
Outputs:
- snr: float32 [16, 1048576], P('tmpl', 'tm')
The draws below stay inside these ranges and needn't reach their ends.
Inputs may be any that keep to these rules, and one draw needn't show every extreme that they name: psd_bins[r, c] names the row of psd_values that serves frequency bin r * 65536 + c.
All inputs are finite; a program needn't handle non-finite values.
Results may differ from the reference program's by a relative error of at most 0.0003.
Values sent between devices are 32-bit elements; how exact they have to be, the bound alone decides.
A program may use at most 128 MiB of HBM per device.

```python
import math
import jax
import jax.numpy as jnp
from jax import lax

SUB = 65536
OR = 32768
R = 8192
LANES = 8
SEGMENTS = 4
ROWS = 32768
HALF_ROWS = 4
TEMPLATES = 16


def draw_psd_bins(key, part):
    frequency = jnp.arange(HALF_ROWS * SUB, dtype=jnp.int32)
    base_row = frequency // (HALF_ROWS * SUB // R)
    jitter = jax.random.randint(key, frequency.shape, 0, 2, dtype=jnp.int32)
    jitter = jnp.where(frequency == 0, 0, jitter)
    return jnp.minimum(base_row + jitter, R - 1).reshape(HALF_ROWS, SUB)


def place_ends(entries, rng, smallest, high):
    extent = entries.shape
    spot = [jax.random.randint(jax.random.fold_in(rng, axis), (), 0, extent[axis]) for axis in range(len(extent))]
    entries = entries.at[tuple(spot)].set(smallest)
    longest = extent.index(max(extent))
    spot[longest] = (spot[longest] + 1) % extent[longest]
    return entries.at[tuple(spot)].set(high)


def block_scale(own_key, shape, pieces, smallest, largest):
    factor_of = 1.0
    for dim, shards_of in pieces:
        draws = jax.random.uniform(jax.random.fold_in(jax.random.fold_in(own_key, 6), dim), (shards_of,), jnp.float32, smallest / len(pieces), largest / len(pieces))
        factor_of = factor_of * jnp.repeat(jnp.exp(draws), shape[dim] // shards_of).reshape((-1,) + (1,) * (len(shape) - 1 - dim))
    return factor_of


def centred(key, shape, scale, bound, cuts=(), kind=jnp.bfloat16):
    loudness = block_scale(key, shape, cuts, -0.22, 0.18) if cuts else 1.0
    drawn = jax.random.normal(key, shape, jnp.float32) * scale * loudness
    return jnp.minimum(jnp.maximum(drawn, -bound), bound).astype(kind)


def setup_inputs(seed: int = 0) -> dict:
    splits = jax.random.split(jax.random.key(seed), 6)
    strain = centred(splits[0], (LANES, SEGMENTS * ROWS), 1.0, 6.0, ((0, 8), (1, 4)), jnp.float32)
    psd_bins = draw_psd_bins(jax.random.fold_in(splits[5], 71), 0)
    psd_values = jnp.clip(jnp.exp(math.log(4.0) - 2.7725887 * jax.random.uniform(splits[2], (SEGMENTS, R), jnp.float32) ** block_scale(splits[2], (SEGMENTS, R), ((0, 4),), -0.2, 0.2)), 0.25, 4.0)
    chirp_slope = place_ends(jax.random.randint(splits[3], (TEMPLATES,), 0, 1024), jax.random.fold_in(splits[3], 1), 0, 1023).astype(jnp.int32)
    chirp_curve = place_ends(jax.random.randint(splits[4], (TEMPLATES,), 1, 64), jax.random.fold_in(splits[4], 1), 1, 63).astype(jnp.int32)
    return {"strain": strain, "psd_bins": psd_bins, "psd_values": psd_values, "chirp_slope": chirp_slope, "chirp_curve": chirp_curve}


TWO_PI = 2.0 * math.pi

def chirp_phase(frequency, slope, curve, modulus):
    high_part = frequency // 1024
    low_part = frequency % 1024
    square = 2 * high_part * low_part % (modulus // 1024) * 1024 + low_part * low_part
    square = square % modulus
    return (slope * frequency + curve * square) % modulus

def template_parts(frequency, chirp_slope, chirp_curve, modulus, k_low, k_cut):
    phase = chirp_phase(frequency[None, :], chirp_slope[:, None], chirp_curve[:, None], modulus)
    angles = phase.astype(jnp.float32) * (TWO_PI / modulus)
    ratio = frequency.astype(jnp.float32) / k_low
    inside = (frequency >= k_low) & (frequency < k_cut)
    amplitude = jnp.where(inside, jnp.power(jnp.maximum(ratio, 1.0), -7.0 / 6.0), 0.0)
    return (amplitude * jnp.cos(angles), -amplitude * jnp.sin(angles))

def reference(strain, psd_bins, psd_values, chirp_slope, chirp_curve):
    lanes = strain.shape[0]
    total_len = SUB * lanes
    half_len = total_len // 2
    intersection = OR * lanes
    stride = ROWS * lanes
    stream = strain.T.reshape(-1)
    padded = jnp.concatenate([jnp.zeros((intersection,), jnp.float32), stream])
    frequency = jnp.arange(half_len, dtype=jnp.int32)
    tmpl_re, tmpl_im = template_parts(frequency, chirp_slope, chirp_curve, total_len, total_len // 200, 3 * total_len // 8)
    power = tmpl_re * tmpl_re + tmpl_im * tmpl_im
    bins = psd_bins.reshape(-1)
    norm_scale = 1.0 / math.sqrt(total_len)

    def one_segment(segment):
        start = (segment * stride).astype(jnp.int32)
        data = lax.dynamic_slice(padded, (start,), (total_len,))
        spectrum = jnp.fft.fft(data)[:half_len]
        inv_psd = 1.0 / jnp.take(psd_values[segment], bins)
        white_re = jnp.real(spectrum) * inv_psd * norm_scale
        white_im = jnp.imag(spectrum) * inv_psd * norm_scale
        coef_re = white_re * tmpl_re + white_im * tmpl_im
        coef_im = white_im * tmpl_re - white_re * tmpl_im
        widths = ((0, 0), (0, total_len - half_len))
        series = jnp.fft.ifft(lax.complex(jnp.pad(coef_re, widths), jnp.pad(coef_im, widths)), axis=-1) * total_len
        sigma_sq = lax.optimization_barrier(jnp.sum(power * inv_psd, axis=-1))
        magnitude = jnp.abs(series) / jnp.sqrt(sigma_sq)[:, None]
        return magnitude[:, intersection:]
    result = lax.map(one_segment, jnp.arange(SEGMENTS, dtype=jnp.int32))
    return jnp.transpose(result, (1, 0, 2)).reshape(result.shape[1], -1)
```

```python
import functools
import math

import jax
import jax.numpy as jnp
import numpy as np
from jax import lax
from jax.experimental import pallas as pl
from jax.experimental.pallas import tpu as pltpu
from jax.sharding import PartitionSpec as P

TWO_PI = 2.0 * math.pi
LANE = 128
FINE = 32
COARSE = 16
VMEM_LIMIT = 63 * 1024 * 1024
BF16 = jnp.bfloat16
F32 = jnp.float32
NN = (((1,), (0,)), ((), ()))
NT = (((1,), (1,)), ((), ()))


def shifted(block, axis, distance):
    devices = range(lax.axis_size(axis))
    route = [(i - distance, i) for i in devices if i - distance in devices]
    return lax.ppermute(block, axis, route)


def factor_table(coarse, fine, cols, modulus, direction):
    index = np.concatenate([np.asarray(coarse), np.asarray(fine)]).astype(np.int64)
    angle = (index[:, None] * np.asarray(cols, dtype=np.int64)[None, :] % modulus) * (
        direction * TWO_PI / modulus
    )
    return jnp.asarray(np.stack([np.cos(angle), np.sin(angle)]).astype(np.float32))


def base_table(rows, cols, modulus, direction):
    return factor_table(FINE * np.arange(rows // FINE), np.arange(FINE), cols, modulus, direction)


def product_rows(table, outer, lanes=slice(None), fine=FINE):
    coarse = table.shape[1] - fine
    c1 = table[0, pl.ds(outer, 1), :][:, lanes]
    s1 = table[1, pl.ds(outer, 1), :][:, lanes]
    c0 = table[0, coarse:, lanes]
    s0 = table[1, coarse:, lanes]
    return c1 * c0 - s1 * s0, s1 * c0 + c1 * s0


def halves(value):
    high = value.astype(BF16)
    return high, (value - high.astype(F32)).astype(BF16)


def put(ref, index, value):
    high, low = halves(value)
    ref[(0,) + index] = high
    ref[(1,) + index] = low


def put_turn(ref, first, rows, lane, lanes, height, width, c, s):
    for part, value in ((0, c), (1, s)):
        high, low = halves(value)
        for slot, piece in ((0, high), (1, low)):
            ref[slot, pl.ds(first + part * height, rows), lane : lane + lanes] = piece
            other = piece if part == 0 else -piece
            ref[slot, pl.ds(first + (1 - part) * height, rows), lane + width : lane + width + lanes] = other


def split_dot(a, b, dims):
    ((a_axis,), (b_axis,)), _ = dims
    left = jnp.concatenate([a[0], a[1], a[0]], axis=a_axis)
    right = jnp.concatenate([b[1], b[0], b[0]], axis=b_axis)
    return lax.dot_general(left, right, dims, preferred_element_type=F32)


def turn(value, numerator, count):
    re, im = value
    step = numerator % count
    if step == 0:
        return re, im
    if 4 * step == count:
        return -im, re
    if 2 * step == count:
        return -re, -im
    if 4 * step == 3 * count:
        return im, -re
    c = math.cos(TWO_PI * step / count)
    s = math.sin(TWO_PI * step / count)
    if 8 * step % count == 0:
        size = math.sqrt(0.5)
        if (c > 0) == (s > 0):
            pair = (re - im) * size, (re + im) * size
        else:
            pair = (re + im) * size, (im - re) * size
        return pair if c > 0 else (-pair[0], -pair[1])
    return re * c - im * s, re * s + im * c


def small_dft(values, direction, wanted):
    count = len(values)
    if count == 1:
        return {0: values[0]}
    half = count // 2
    result = {}
    for odd in (0, 1):
        inner_wanted = [w // 2 for w in wanted if w % 2 == odd]
        if not inner_wanted:
            continue
        folded = []
        for j in range(half):
            (a, b), (c, d) = values[j], values[j + half]
            if odd:
                folded.append(turn((a - c, b - d), direction * j, count))
            else:
                folded.append((a + c, b + d))
        for w, value in small_dft(folded, direction, inner_wanted).items():
            result[2 * w + odd] = value
    return result


def look_up(bins, table_ref):
    high = bins // LANE
    low = bins % LANE

    def body(row, total):
        lanes = pl.ds(pl.multiple_of(row * LANE, LANE), LANE)
        line = jnp.broadcast_to(table_ref[:, lanes], bins.shape)
        return jnp.where(
            high == row,
            jnp.take_along_axis(line, low, axis=1, mode="promise_in_bounds"),
            total,
        )

    picked = lax.fori_loop(
        0, table_ref.shape[1] // LANE, body, jnp.ones(bins.shape, F32), unroll=4
    )
    return 1.0 / picked


def density_rows(bins_ref, ordered_ref, bands, inner):
    member_rows = bins_ref.shape[1] // inner
    for q in range(inner // LANE):
        for band in range(bands):
            for row in range(member_rows):
                start = row * inner + q * LANE
                target = (q * bands + band) * member_rows + row
                ordered_ref[target : target + 1, :] = bins_ref[
                    band : band + 1, start : start + LANE
                ]


def density_kernel(bands, inner, bins_ref, table_ref, out_ref, ordered_ref):
    density_rows(bins_ref, ordered_ref, bands, inner)
    out_ref[...] = look_up(ordered_ref[...], table_ref)


def amplitude_rows(first, fold, reach, shape, total_len):
    k_low = total_len // 200
    k_cut = 3 * total_len // 8
    member = first // reach
    row = fold * (first - member * reach + lax.broadcasted_iota(jnp.int32, shape, 0)) + member
    frequency = row * shape[1] + lax.broadcasted_iota(jnp.int32, shape, 1)
    ratio = jnp.maximum(frequency.astype(F32) / k_low, 1.0)
    inside = (frequency >= k_low) & (frequency < k_cut)
    return jnp.where(inside, jnp.exp(jnp.log(ratio) * (-7.0 / 6.0)), 0.0)


def template_rows(slope_ref, curve_ref, chirp_ref, m, total_len):
    inner = chirp_ref.shape[3]
    fold = (chirp_ref.shape[2] - COARSE) // 8
    for first in range(0, COARSE + 8 * fold, 8):
        slope = slope_ref[m]
        curve = curve_ref[m]
        shape = (8, inner)
        row = lax.broadcasted_iota(jnp.int32, shape, 0)
        column = lax.broadcasted_iota(jnp.int32, shape, 1)
        mask = total_len - 1
        if first < COARSE:
            far = (8 * fold * inner) * (first + row)
            phase = slope * far + curve * ((2 * far * column) & mask)
        else:
            near = inner * (fold * row + (first - COARSE) // 8) + column
            phase = slope * near + curve * ((near * near) & mask)
        angle = (phase & mask).astype(F32) * (TWO_PI / total_len)
        chirp_ref[m, 0, first : first + 8, :] = jnp.cos(angle)
        chirp_ref[m, 1, first : first + 8, :] = jnp.sin(angle)


def amplitude_table(amp_ref, fold, total_len):
    depth, inner = amp_ref.shape
    reach = depth // fold

    @pl.loop(0, depth // 8)
    def _(i):
        first = pl.multiple_of(i * 8, 8)
        amp_ref[pl.ds(first, 8), :] = amplitude_rows(first, fold, reach, (8, inner), total_len)


def table_kernel(total_len, slope_ref, curve_ref, chirp_ref, amp_ref):
    for m in range(chirp_ref.shape[0]):
        template_rows(slope_ref, curve_ref, chirp_ref, m, total_len)
    amplitude_table(amp_ref, (chirp_ref.shape[2] - COARSE) // 8, total_len)


def gather_kernel(
    bands, inner, total_len,
    own_ref, bins_ref, table_ref, slope_ref, curve_ref,
    out_ref, chirp_ref, amp_ref,
    ordered_ref, send_sem, recv_sem, tail_send, tail_recv,
):
    tm = lax.axis_index("tm")
    me = lax.axis_index("tmpl")
    count = lax.axis_size("tm")
    half = own_ref.shape[0]
    extra = ordered_ref.shape[0]

    def peer(distance):
        low = me % (2 * distance)
        return me - low + (low + distance) % (2 * distance)

    core = peer(1)
    side = peer(2)
    front = peer(4)
    side_front = side + front - me
    spans = ((half, half), (0, half), (2 * half, extra))

    barrier = pltpu.get_barrier_semaphore()
    for other in (core, side, front):
        pl.semaphore_signal(
            barrier, inc=1, device_id={"tmpl": other}, device_id_type=pl.DeviceIdType.MESH
        )

    for other in ((tm + 1) % count, (tm + count - 1) % count):
        pl.semaphore_signal(
            barrier, inc=1, device_id={"tm": other}, device_id_type=pl.DeviceIdType.MESH
        )
    pl.semaphore_wait(barrier, 5)

    def copy(part, kind, slot, piece, target, source=None):
        first, rows = spans[part]
        if part == 1 and kind in (1, 2):
            piece = 2 - kind
        if piece is not None:
            rows = rows // 2
            first = first + piece * rows
        view = out_ref.at[slot, pl.ds(first, rows), :]
        return pltpu.make_async_remote_copy(
            src_ref=view if source is None else source,
            dst_ref=view,
            send_sem=send_sem.at[part, kind],
            recv_sem=recv_sem.at[part, kind],
            device_id={"tmpl": target},
            device_id_type=pl.DeviceIdType.MESH,
        )

    def send(part, kind, source=None):
        slot, piece, target = (
            (me, None, core), (me, None, side), (me, None, front),
            (side, None, core), (front, None, core),
            (side, 0, front), (front, 1, side),
            (side_front, 0, core), (side_front, 1, core),
        )[kind]
        return copy(part, kind, slot, piece, target, source if kind < 3 else None)

    def first_stage(part, source=None):
        send(part, 1, source).start()
        send(part, 2, source).start()
        send(part, 0, source).start()

    def second_stage(part):
        copy(part, 1, side, None, side).wait_recv()
        send(part, 5).start()
        copy(part, 2, front, None, front).wait_recv()
        send(part, 6).start()
        send(part, 3).start()
        send(part, 4).start()

    def third_stage(part):
        copy(part, 5, side_front, 0, front).wait_recv()
        send(part, 7).start()
        copy(part, 6, side_front, 1, side).wait_recv()
        send(part, 8).start()

    def last_stage(part, source=None):
        other = core + side - me
        across = core + front - me
        corner = core + side_front - me
        copy(part, 0, core, None, core).wait_recv()
        copy(part, 3, other, None, core).wait_recv()
        copy(part, 4, across, None, core).wait_recv()
        copy(part, 7, corner, 0, core).wait_recv()
        copy(part, 8, corner, 1, core).wait_recv()
        for kind in range(9):
            if part != 1 or kind not in (5, 6):
                send(part, kind, source).wait_send()

    def onward(kind):
        slot, piece = ((me, None), (side, 0), (front, 1), (side_front, 0), (side_front, 1))[kind]
        rows = half if piece is None else half // 2
        first = 0 if piece is None else piece * rows
        source = own_ref if kind == 0 else out_ref.at[slot, pl.ds(half + first, rows), :]
        return pltpu.make_async_remote_copy(
            src_ref=source,
            dst_ref=out_ref.at[slot, pl.ds(first, rows), :],
            send_sem=tail_send.at[kind],
            recv_sem=tail_recv.at[kind],
            device_id={"tm": (tm + 1) % count},
            device_id_type=pl.DeviceIdType.MESH,
        )

    def pass_on(kinds):
        @pl.when(tm < count - 1)
        def _():
            for kind in kinds:
                onward(kind).start()

    def second_stage_old():
        copy(1, 1, side, None, side).wait_recv()
        onward(1).wait_recv()
        send(1, 3).start()
        copy(1, 2, front, None, front).wait_recv()
        onward(2).wait_recv()
        send(1, 4).start()

    def third_stage_old():
        onward(3).wait_recv()
        send(1, 7).start()
        onward(4).wait_recv()
        send(1, 8).start()

    pass_on((0,))
    first_stage(0, own_ref)
    out_ref[me, half : 2 * half, :] = own_ref[...]
    density_rows(bins_ref, ordered_ref, bands, inner)
    third = extra // 3

    def densities(i):
        rows = slice(i * third, (i + 1) * third)
        out_ref[me, 2 * half + i * third : 2 * half + (i + 1) * third, :] = look_up(
            ordered_ref[rows, :], table_ref
        )

    @pl.when(tm == 0)
    def _():
        for slot in range(out_ref.shape[0]):
            out_ref[slot, :half, :] = jnp.zeros((half, LANE), F32)

    @pl.when(tm > 0)
    def _():
        onward(0).wait_recv()
        first_stage(1)

    densities(0)
    second_stage(0)
    pass_on((1, 2))
    densities(1)
    third_stage(0)
    pass_on((3, 4))
    densities(2)
    first_stage(2)

    @pl.when(tm > 0)
    def _():
        second_stage_old()

    template_rows(slope_ref, curve_ref, chirp_ref, 0, total_len)
    second_stage(2)

    @pl.when(tm > 0)
    def _():
        third_stage_old()

    for m in range(1, chirp_ref.shape[0]):
        template_rows(slope_ref, curve_ref, chirp_ref, m, total_len)
    third_stage(2)
    amplitude_table(amp_ref, (chirp_ref.shape[2] - COARSE) // 8, total_len)
    last_stage(0, own_ref)

    @pl.when(tm > 0)
    def _():
        last_stage(1)

    last_stage(2)

    @pl.when(tm < count - 1)
    def _():
        for kind in range(5):
            onward(kind).wait_send()


def filter_kernel(
    segment_rows, member_rows, bands, templates, scale,
    packed_ref, amp_ref, chirp_ref, f1_ref, twist1_ref, f2_ref, i1_ref, twist2_ref, i2_ref,
    out_ref,
    f1_buf, x_buf, f2_buf, y_buf, part_ref, weight_ref, c_buf, i1_buf, i2_buf, g_buf,
):
    groups = packed_ref.shape[0]
    inner = amp_ref.shape[1]
    half = inner // 2
    fold = c_buf.shape[1]
    reach = amp_ref.shape[0] // fold
    band_rows = LANE // fold

    for a in range(2):
        for outer in range(half // FINE):
            for lane in range(0, half, LANE):
                c, s = product_rows(f1_ref, outer, slice(a * half + lane, a * half + lane + LANE))
                put(f1_buf.at[a], (slice(outer * FINE, (outer + 1) * FINE), slice(lane, lane + LANE)), c)
                put(
                    f1_buf.at[a],
                    (slice(half + outer * FINE, half + (outer + 1) * FINE), slice(lane, lane + LANE)),
                    s,
                )
    for j in range(groups):
        for a in range(fold):
            c, s = product_rows(f2_ref, a, slice(j * LANE, (j + 1) * LANE), band_rows)
            put_turn(f2_buf.at[j], a * band_rows, band_rows, 0, LANE, LANE, LANE, c, s)

    for pair in range(groups // 2):
        for a in range(2):
            for side in range(2):
                j = 2 * pair + side
                for first in range(0, half, FINE):
                    value = packed_ref[j, pl.ds(2 * first + a, FINE, stride=2), :]
                    put(
                        x_buf.at[pair % x_buf.shape[0], a],
                        (slice(first, first + FINE), slice(side * LANE, (side + 1) * LANE)),
                        value,
                    )
        even = split_dot(f1_buf.at[0], x_buf.at[pair % x_buf.shape[0], 0], NN)
        odd = split_dot(f1_buf.at[1], x_buf.at[pair % x_buf.shape[0], 1], NN)
        for block in range(half // FINE):
            rows = slice(block * FINE, (block + 1) * FINE)
            lower = slice(half + block * FINE, half + (block + 1) * FINE)
            for side in range(2):
                j = 2 * pair + side
                lanes = slice(side * LANE, (side + 1) * LANE)
                for r in range(2):
                    c, s = product_rows(
                        twist1_ref, r * (half // FINE) + block, slice(j * LANE, (j + 1) * LANE)
                    )
                    if r:
                        a, b = even[rows, lanes] - odd[rows, lanes], even[lower, lanes] - odd[lower, lanes]
                    else:
                        a, b = even[rows, lanes] + odd[rows, lanes], even[lower, lanes] + odd[lower, lanes]
                    target = slice(r * half + block * FINE, r * half + (block + 1) * FINE)
                    put(y_buf.at[j % y_buf.shape[0]], (target, slice(0, LANE)), a * c - b * s)
                    put(y_buf.at[j % y_buf.shape[0]], (target, slice(LANE, 2 * LANE)), a * s + b * c)
        for side in range(2):
            j = 2 * pair + side
            part_ref[j] = split_dot(f2_buf.at[j], y_buf.at[j % y_buf.shape[0]], NT)

    for q in range(inner // LANE):
        for band in range(bands):
            for j in range(groups):
                source = segment_rows + (q * bands + band) * member_rows
                target = (band * groups + j) * member_rows
                weight_ref[q, target : target + member_rows, :] = packed_ref[
                    j, source : source + member_rows, :
                ]

    for a in range(fold):
        @pl.loop(0, 1)
        def _(_):
            zero = jnp.zeros((LANE - reach, inner), BF16)
            for m in range(templates):
                for slot in range(2):
                    c_buf[m, a, slot, reach:LANE, :] = zero
                    c_buf[m, a, slot, LANE + reach :, :] = zero

    total = jnp.zeros((8, LANE), F32)
    for a in range(fold):
        for q0 in range(0, band_rows, COARSE):
            rows = slice(a * band_rows + q0, a * band_rows + q0 + COARSE)
            lower = slice(LANE + a * band_rows + q0, LANE + a * band_rows + q0 + COARSE)
            for lane in range(0, inner, LANE):
                lanes = slice(lane, lane + LANE)
                values = [
                    (part_ref[j, rows, lanes], part_ref[j, lower, lanes]) for j in range(groups)
                ]
                sums = small_dft(values, -1, list(range(bands)))
                for band in range(bands):
                    b = band * band_rows + q0
                    amp = amp_ref[a * reach + b : a * reach + b + COARSE, lanes]
                    density = weight_ref[lane // LANE, pl.ds(a + fold * b, COARSE, stride=fold), :]
                    weight = amp * density
                    power = weight * amp
                    total = total + power[:8] + power[8:]
                    weight = weight * scale
                    x_re = sums[band][0] * weight
                    x_im = sums[band][1] * weight
                    for m in range(templates):
                        cs, ss = [], []
                        for n in range(b // 8, b // 8 + COARSE // 8):
                            c1 = chirp_ref[m, 0, n : n + 1, lanes]
                            s1 = chirp_ref[m, 1, n : n + 1, lanes]
                            near = slice(COARSE + 8 * a, COARSE + 8 * (a + 1))
                            c0 = chirp_ref[m, 0, near, lanes]
                            s0 = chirp_ref[m, 1, near, lanes]
                            cs.append(c1 * c0 - s1 * s0)
                            ss.append(s1 * c0 + c1 * s0)
                        c = jnp.concatenate(cs, axis=0)
                        s = jnp.concatenate(ss, axis=0)
                        put(c_buf.at[m, a], (slice(b, b + COARSE), lanes), x_re * c - x_im * s)
                        put(
                            c_buf.at[m, a],
                            (slice(LANE + b, LANE + b + COARSE), lanes),
                            x_re * s + x_im * c,
                        )
    total = jnp.sum(jnp.sum(total, axis=0, keepdims=True), axis=1, keepdims=True)
    norm = 1.0 / jnp.sqrt(total)

    height = i2_buf.shape[2] // 2
    steps = half // LANE
    for rho in range(2):
        for outer in range(height // FINE):
            c, s = product_rows(i2_ref, rho * (height // FINE) + outer)
            put_turn(i2_buf.at[rho], outer * FINE, FINE, 0, half, height, half, c, s)

    per_step = LANE // FINE
    row_stride = 2 * templates * fold * steps

    @pl.loop(0, steps)
    def _(h):
        for a in range(fold):
            for o in range(per_step):
                c, s = product_rows(i1_ref, h * per_step + o, slice(a * LANE, (a + 1) * LANE))
                put_turn(i1_buf.at[a], o * FINE, FINE, 0, LANE, LANE, LANE, c, s)
        for m in range(templates):
            mixed = [split_dot(i1_buf.at[a], c_buf.at[m, a], NN) for a in range(fold)]
            for o in range(per_step):
                rows = slice(o * FINE, (o + 1) * FINE)
                lower = slice(LANE + o * FINE, LANE + (o + 1) * FINE)
                for lane in range(0, half, LANE):
                    sides = []
                    for first in (lane, half + lane):
                        lanes = slice(first, first + LANE)
                        values = [(mixed[a][rows, lanes], mixed[a][lower, lanes]) for a in range(fold)]
                        outs = small_dft(values, 1, list(range(fold)))
                        turned = []
                        for r in range(fold):
                            c, s = product_rows(
                                twist2_ref, (r * steps + h) * per_step + o, lanes
                            )
                            a, b = outs[r]
                            turned.append((a * c - b * s, a * s + b * c))
                        sides.append(turned)
                    for r in range(fold):
                        target = slice(r * LANE + o * FINE, r * LANE + (o + 1) * FINE)
                        for part in range(2):
                            near, far = sides[0][r][part], sides[1][r][part]
                            lanes = slice(part * half + lane, part * half + lane + LANE)
                            put(g_buf.at[m, 0], (target, lanes), near + far)
                            put(g_buf.at[m, 1], (target, lanes), near - far)
            for rho in range(2):
                z = split_dot(i2_buf.at[rho], g_buf.at[m, rho], NT)
                z_re, z_im = z[:height], z[height:]
                size = jnp.sqrt(z_re * z_re + z_im * z_im) * norm
                for r in range(fold):
                    first = ((rho * fold + r) * steps + h) * templates + m
                    out_ref[pl.ds(first, height, stride=row_stride), :] = size[:, r * LANE : (r + 1) * LANE]


def local(strain, psd_bins, psd_values, chirp_slope, chirp_curve):
    groups = lax.axis_size("tmpl")
    own_part = strain[0]
    half_len = own_part.shape[0]
    sub_len = 2 * half_len
    total_len = sub_len * groups
    inner = sub_len // LANE
    outer = total_len // inner
    depth = 3 * outer // 8
    k_low = total_len // 200
    k_cut = 3 * total_len // 8
    bands = 3 * groups // 8
    templates = chirp_slope.shape[0]
    member_len = psd_bins.shape[1]
    member_rows = member_len // inner
    fold = outer // (2 * LANE)
    reach = depth // fold
    assert (fold * inner) ** 2 % total_len == 0 and 2 * fold * inner**2 % total_len == 0
    assert total_len & (total_len - 1) == 0 and reach <= 8 * COARSE and reach <= LANE

    extra = bands * member_len // LANE
    table_shapes = [
        jax.ShapeDtypeStruct((templates, 2, COARSE + 8 * fold, inner), F32),
        jax.ShapeDtypeStruct((depth, inner), F32),
    ]
    vmem = pl.BlockSpec(memory_space=pltpu.VMEM)
    smem = pl.BlockSpec(memory_space=pltpu.SMEM)
    own_rows = own_part.reshape(-1, LANE)
    rows = 2 * own_rows.shape[0] + extra
    if groups == 8:
        packed, chirp, amplitude = pl.pallas_call(
            functools.partial(gather_kernel, bands, inner, total_len),
            in_specs=[vmem, vmem, vmem, smem, smem],
            out_specs=[vmem, vmem, vmem],
            out_shape=[jax.ShapeDtypeStruct((groups, rows, LANE), F32)] + table_shapes,
            scratch_shapes=[
                pltpu.VMEM((extra, LANE), jnp.int32),
                pltpu.SemaphoreType.DMA((3, 9)),
                pltpu.SemaphoreType.DMA((3, 9)),
                pltpu.SemaphoreType.DMA((5,)),
                pltpu.SemaphoreType.DMA((5,)),
            ],
            compiler_params=pltpu.CompilerParams(collective_id=0, has_side_effects=True),
            name="gather",
        )(own_rows, psd_bins, psd_values, chirp_slope, chirp_curve)
    else:
        tail = shifted(own_part, "tm", 1).reshape(-1, LANE)
        inv_psd = pl.pallas_call(
            functools.partial(density_kernel, bands, inner),
            out_shape=jax.ShapeDtypeStruct((extra, LANE), F32),
            scratch_shapes=[pltpu.VMEM((extra, LANE), jnp.int32)],
            name="density",
        )(psd_bins, psd_values)
        packed = lax.all_gather(
            jnp.concatenate([tail, own_rows, inv_psd], axis=0), "tmpl", axis=0, tiled=False
        )
        chirp, amplitude = pl.pallas_call(
            functools.partial(table_kernel, total_len),
            in_specs=[smem, smem],
            out_shape=table_shapes,
            name="tables",
        )(chirp_slope, chirp_curve)

    half = inner // 2
    place = np.arange(outer)
    sample = (place % LANE) * groups + place // LANE
    step = np.arange(half)
    band_rows = LANE // fold
    f1 = base_table(half, np.concatenate([2 * step, 2 * step + 1]), inner, -1.0)
    twist1 = base_table(inner, sample, total_len, -1.0)
    f2 = factor_table(np.arange(fold), fold * np.arange(band_rows), sample, outer, -1.0)
    member = np.arange(fold)[:, None] + fold * np.arange(LANE)[None, :]
    i1 = base_table(2 * LANE, member.reshape(-1), outer, 1.0)
    twist2 = base_table(outer, np.arange(inner), total_len, 1.0)
    late = half + np.arange(2)[:, None] + 2 * FINE * np.arange(half // 2 // FINE)[None, :]
    i2 = factor_table(late.reshape(-1), 2 * np.arange(FINE), step, inner, 1.0)

    out_rows = half * (outer // LANE) * templates
    flat = pl.pallas_call(
        functools.partial(
            filter_kernel, inner, member_rows, bands, templates, 1.0 / math.sqrt(total_len)
        ),
        in_specs=[vmem] * 9,
        out_specs=vmem,
        out_shape=jax.ShapeDtypeStruct((out_rows, LANE), F32),
        scratch_shapes=[
            pltpu.VMEM((2, 2, inner, half), BF16),
            pltpu.VMEM((2, 2, 2, half, 2 * LANE), BF16),
            pltpu.VMEM((groups, 2, 2 * LANE, 2 * LANE), BF16),
            pltpu.VMEM((4, 2, inner, 2 * LANE), BF16),
            pltpu.VMEM((groups, 2 * LANE, inner), F32),
            pltpu.VMEM((inner // LANE, depth, LANE), F32),
            pltpu.VMEM((templates, fold, 2, 2 * LANE, inner), BF16),
            pltpu.VMEM((fold, 2, 2 * LANE, 2 * LANE), BF16),
            pltpu.VMEM((2, 2, half, inner), BF16),
            pltpu.VMEM((templates, 2, 2, fold * LANE, inner), BF16),
        ],
        compiler_params=pltpu.CompilerParams(vmem_limit_bytes=VMEM_LIMIT),
        name="filter",
    )(packed, amplitude, chirp, f1, twist1, f2, i1, twist2, i2)
    result = flat.reshape(-1, templates, LANE)
    return jnp.transpose(result, (1, 0, 2)).reshape(templates, -1)


def solution(mesh):
    placed = (P("tmpl", "tm"), P(None, "tmpl"), P("tm", None), P("tmpl"), P("tmpl"))
    return jax.shard_map(
        local, mesh=mesh, in_specs=placed, out_specs=P("tmpl", "tm"), check_vma=False
    )
```

```python
import functools
import math

import jax
import jax.numpy as jnp
import numpy as np
from jax import lax
from jax.experimental import pallas as pl
from jax.experimental.pallas import tpu as pltpu
from jax.sharding import PartitionSpec as P

TWO_PI = 2.0 * math.pi
LANE = 128
FINE = 32
COARSE = 16
VMEM_LIMIT = 63 * 1024 * 1024
BF16 = jnp.bfloat16
F32 = jnp.float32
NN = (((1,), (0,)), ((), ()))
NT = (((1,), (1,)), ((), ()))


def shifted(block, axis, distance):
    devices = range(lax.axis_size(axis))
    route = [(i - distance, i) for i in devices if i - distance in devices]
    return lax.ppermute(block, axis, route)


def factor_table(coarse, fine, cols, modulus, direction):
    index = np.concatenate([np.asarray(coarse), np.asarray(fine)]).astype(np.int64)
    angle = (index[:, None] * np.asarray(cols, dtype=np.int64)[None, :] % modulus) * (
        direction * TWO_PI / modulus
    )
    return jnp.asarray(np.stack([np.cos(angle), np.sin(angle)]).astype(np.float32))


def base_table(rows, cols, modulus, direction):
    return factor_table(FINE * np.arange(rows // FINE), np.arange(FINE), cols, modulus, direction)


def product_rows(table, outer, lanes=slice(None), fine=FINE):
    coarse = table.shape[1] - fine
    c1 = table[0, pl.ds(outer, 1), :][:, lanes]
    s1 = table[1, pl.ds(outer, 1), :][:, lanes]
    c0 = table[0, coarse:, lanes]
    s0 = table[1, coarse:, lanes]
    return c1 * c0 - s1 * s0, s1 * c0 + c1 * s0


def halves(value):
    high = value.astype(BF16)
    return high, (value - high.astype(F32)).astype(BF16)


def put(ref, index, value):
    high, low = halves(value)
    ref[(0,) + index] = high
    ref[(1,) + index] = low


def put_turn(ref, first, rows, lane, lanes, height, width, c, s):
    for part, value in ((0, c), (1, s)):
        high, low = halves(value)
        for slot, piece in ((0, high), (1, low)):
            ref[slot, pl.ds(first + part * height, rows), lane : lane + lanes] = piece
            other = piece if part == 0 else -piece
            ref[slot, pl.ds(first + (1 - part) * height, rows), lane + width : lane + width + lanes] = other


def split_dot(a, b, dims):
    ((a_axis,), (b_axis,)), _ = dims
    left = jnp.concatenate([a[0], a[1], a[0]], axis=a_axis)
    right = jnp.concatenate([b[1], b[0], b[0]], axis=b_axis)
    return lax.dot_general(left, right, dims, preferred_element_type=F32)


def turn(value, numerator, count):
    re, im = value
    step = numerator % count
    if step == 0:
        return re, im
    if 4 * step == count:
        return -im, re
    if 2 * step == count:
        return -re, -im
    if 4 * step == 3 * count:
        return im, -re
    c = math.cos(TWO_PI * step / count)
    s = math.sin(TWO_PI * step / count)
    if 8 * step % count == 0:
        size = math.sqrt(0.5)
        if (c > 0) == (s > 0):
            pair = (re - im) * size, (re + im) * size
        else:
            pair = (re + im) * size, (im - re) * size
        return pair if c > 0 else (-pair[0], -pair[1])
    return re * c - im * s, re * s + im * c


def small_dft(values, direction, wanted):
    count = len(values)
    if count == 1:
        return {0: values[0]}
    half = count // 2
    result = {}
    for odd in (0, 1):
        inner_wanted = [w // 2 for w in wanted if w % 2 == odd]
        if not inner_wanted:
            continue
        folded = []
        for j in range(half):
            (a, b), (c, d) = values[j], values[j + half]
            if odd:
                folded.append(turn((a - c, b - d), direction * j, count))
            else:
                folded.append((a + c, b + d))
        for w, value in small_dft(folded, direction, inner_wanted).items():
            result[2 * w + odd] = value
    return result


def look_up(bins, table_ref):
    high = bins // LANE
    low = bins % LANE

    def body(row, total):
        lanes = pl.ds(pl.multiple_of(row * LANE, LANE), LANE)
        line = jnp.broadcast_to(table_ref[:, lanes], bins.shape)
        return jnp.where(
            high == row,
            jnp.take_along_axis(line, low, axis=1, mode="promise_in_bounds"),
            total,
        )

    picked = lax.fori_loop(
        0, table_ref.shape[1] // LANE, body, jnp.ones(bins.shape, F32), unroll=4
    )
    return 1.0 / picked


def density_rows(bins_ref, ordered_ref, bands, inner):
    member_rows = bins_ref.shape[1] // inner
    for q in range(inner // LANE):
        for band in range(bands):
            for row in range(member_rows):
                start = row * inner + q * LANE
                target = (q * bands + band) * member_rows + row
                ordered_ref[target : target + 1, :] = bins_ref[
                    band : band + 1, start : start + LANE
                ]


def density_kernel(bands, inner, bins_ref, table_ref, out_ref, ordered_ref):
    density_rows(bins_ref, ordered_ref, bands, inner)
    out_ref[...] = look_up(ordered_ref[...], table_ref)


def amplitude_rows(first, fold, reach, shape, total_len):
    k_low = total_len // 200
    k_cut = 3 * total_len // 8
    member = first // reach
    row = fold * (first - member * reach + lax.broadcasted_iota(jnp.int32, shape, 0)) + member
    frequency = row * shape[1] + lax.broadcasted_iota(jnp.int32, shape, 1)
    ratio = jnp.maximum(frequency.astype(F32) / k_low, 1.0)
    inside = (frequency >= k_low) & (frequency < k_cut)
    return jnp.where(inside, jnp.exp(jnp.log(ratio) * (-7.0 / 6.0)), 0.0)


def template_rows(slope_ref, curve_ref, chirp_ref, m, total_len):
    inner = chirp_ref.shape[3]
    fold = (chirp_ref.shape[2] - COARSE) // 8
    for first in range(0, COARSE + 8 * fold, 8):
        slope = slope_ref[m]
        curve = curve_ref[m]
        shape = (8, inner)
        row = lax.broadcasted_iota(jnp.int32, shape, 0)
        column = lax.broadcasted_iota(jnp.int32, shape, 1)
        mask = total_len - 1
        if first < COARSE:
            far = (8 * fold * inner) * (first + row)
            phase = slope * far + curve * ((2 * far * column) & mask)
        else:
            near = inner * (fold * row + (first - COARSE) // 8) + column
            phase = slope * near + curve * ((near * near) & mask)
        angle = (phase & mask).astype(F32) * (TWO_PI / total_len)
        chirp_ref[m, 0, first : first + 8, :] = jnp.cos(angle)
        chirp_ref[m, 1, first : first + 8, :] = jnp.sin(angle)


def amplitude_table(amp_ref, fold, total_len):
    depth, inner = amp_ref.shape
    reach = depth // fold

    @pl.loop(0, depth // 8)
    def _(i):
        first = pl.multiple_of(i * 8, 8)
        amp_ref[pl.ds(first, 8), :] = amplitude_rows(first, fold, reach, (8, inner), total_len)


def table_kernel(total_len, slope_ref, curve_ref, chirp_ref, amp_ref):
    for m in range(chirp_ref.shape[0]):
        template_rows(slope_ref, curve_ref, chirp_ref, m, total_len)
    amplitude_table(amp_ref, (chirp_ref.shape[2] - COARSE) // 8, total_len)


def gather_kernel(
    bands, inner, total_len,
    own_ref, bins_ref, table_ref, slope_ref, curve_ref,
    out_ref, chirp_ref, amp_ref,
    ordered_ref, send_sem, recv_sem, tail_send, tail_recv,
):
    tm = lax.axis_index("tm")
    me = lax.axis_index("tmpl")
    count = lax.axis_size("tm")
    half = own_ref.shape[0]
    extra = ordered_ref.shape[0]

    def peer(distance):
        low = me % (2 * distance)
        return me - low + (low + distance) % (2 * distance)

    core = peer(1)
    side = peer(2)
    front = peer(4)
    side_front = side + front - me
    spans = ((half, half), (0, half), (2 * half, extra))

    barrier = pltpu.get_barrier_semaphore()
    for other in (core, side, front):
        pl.semaphore_signal(
            barrier, inc=1, device_id={"tmpl": other}, device_id_type=pl.DeviceIdType.MESH
        )

    for other in ((tm + 1) % count, (tm + count - 1) % count):
        pl.semaphore_signal(
            barrier, inc=1, device_id={"tm": other}, device_id_type=pl.DeviceIdType.MESH
        )
    pl.semaphore_wait(barrier, 5)

    def copy(part, kind, slot, piece, target, source=None):
        first, rows = spans[part]
        if part == 1 and kind in (1, 2):
            piece = 2 - kind
        if piece is not None:
            rows = rows // 2
            first = first + piece * rows
        view = out_ref.at[slot, pl.ds(first, rows), :]
        return pltpu.make_async_remote_copy(
            src_ref=view if source is None else source,
            dst_ref=view,
            send_sem=send_sem.at[part, kind],
            recv_sem=recv_sem.at[part, kind],
            device_id={"tmpl": target},
            device_id_type=pl.DeviceIdType.MESH,
        )

    def send(part, kind, source=None):
        slot, piece, target = (
            (me, None, core), (me, None, side), (me, None, front),
            (side, None, core), (front, None, core),
            (side, 0, front), (front, 1, side),
            (side_front, 0, core), (side_front, 1, core),
        )[kind]
        return copy(part, kind, slot, piece, target, source if kind < 3 else None)

    def first_stage(part, source=None):
        send(part, 1, source).start()
        send(part, 2, source).start()
        send(part, 0, source).start()

    def second_stage(part):
        copy(part, 1, side, None, side).wait_recv()
        send(part, 5).start()
        copy(part, 2, front, None, front).wait_recv()
        send(part, 6).start()
        send(part, 3).start()
        send(part, 4).start()

    def third_stage(part):
        copy(part, 5, side_front, 0, front).wait_recv()
        send(part, 7).start()
        copy(part, 6, side_front, 1, side).wait_recv()
        send(part, 8).start()

    def last_stage(part, source=None):
        other = core + side - me
        across = core + front - me
        corner = core + side_front - me
        copy(part, 0, core, None, core).wait_recv()
        copy(part, 3, other, None, core).wait_recv()
        copy(part, 4, across, None, core).wait_recv()
        copy(part, 7, corner, 0, core).wait_recv()
        copy(part, 8, corner, 1, core).wait_recv()
        for kind in range(9):
            if part != 1 or kind not in (5, 6):
                send(part, kind, source).wait_send()

    def onward(kind):
        slot, piece = ((me, None), (side, 0), (front, 1), (side_front, 0), (side_front, 1))[kind]
        rows = half if piece is None else half // 2
        first = 0 if piece is None else piece * rows
        source = own_ref if kind == 0 else out_ref.at[slot, pl.ds(half + first, rows), :]
        return pltpu.make_async_remote_copy(
            src_ref=source,
            dst_ref=out_ref.at[slot, pl.ds(first, rows), :],
            send_sem=tail_send.at[kind],
            recv_sem=tail_recv.at[kind],
            device_id={"tm": (tm + 1) % count},
            device_id_type=pl.DeviceIdType.MESH,
        )

    def pass_on(kinds):
        @pl.when(tm < count - 1)
        def _():
            for kind in kinds:
                onward(kind).start()

    def second_stage_old():
        copy(1, 1, side, None, side).wait_recv()
        onward(1).wait_recv()
        send(1, 3).start()
        copy(1, 2, front, None, front).wait_recv()
        onward(2).wait_recv()
        send(1, 4).start()

    def third_stage_old():
        onward(3).wait_recv()
        send(1, 7).start()
        onward(4).wait_recv()
        send(1, 8).start()

    pass_on((0,))
    first_stage(0, own_ref)
    out_ref[me, half : 2 * half, :] = own_ref[...]
    density_rows(bins_ref, ordered_ref, bands, inner)
    out_ref[me, 2 * half : 2 * half + extra, :] = look_up(ordered_ref[...], table_ref)
    first_stage(2)
    fold = (chirp_ref.shape[2] - COARSE) // 8

    @pl.when(tm == 0)
    def _():
        for slot in range(out_ref.shape[0]):
            out_ref[slot, :half, :] = jnp.zeros((half, LANE), F32)

    template_rows(slope_ref, curve_ref, chirp_ref, 0, total_len)
    @pl.when(tm > 0)
    def _():
        onward(0).wait_recv()
        first_stage(1)

    second_stage(0)
    pass_on((1, 2))
    third_stage(0)
    pass_on((3, 4))
    second_stage(2)
    for m in range(1, chirp_ref.shape[0]):
        template_rows(slope_ref, curve_ref, chirp_ref, m, total_len)
    third_stage(2)
    @pl.when(tm > 0)
    def _():
        second_stage_old()

    @pl.when(tm > 0)
    def _():
        third_stage_old()

    amplitude_table(amp_ref, fold, total_len)
    last_stage(0, own_ref)

    @pl.when(tm > 0)
    def _():
        last_stage(1)

    last_stage(2)

    @pl.when(tm < count - 1)
    def _():
        for kind in range(5):
            onward(kind).wait_send()


def filter_kernel(
    segment_rows, member_rows, bands, templates, scale,
    packed_ref, amp_ref, chirp_ref, f1_ref, twist1_ref, f2_ref, i1_ref, twist2_ref, i2_ref,
    out_ref,
    f1_buf, x_buf, f2_buf, y_buf, part_ref, weight_ref, c_buf, i1_buf, i2_buf, g_buf,
):
    groups = packed_ref.shape[0]
    inner = amp_ref.shape[1]
    half = inner // 2
    fold = c_buf.shape[1]
    reach = amp_ref.shape[0] // fold
    band_rows = LANE // fold

    for a in range(2):
        for outer in range(half // FINE):
            for lane in range(0, half, LANE):
                c, s = product_rows(f1_ref, outer, slice(a * half + lane, a * half + lane + LANE))
                put(f1_buf.at[a], (slice(outer * FINE, (outer + 1) * FINE), slice(lane, lane + LANE)), c)
                put(
                    f1_buf.at[a],
                    (slice(half + outer * FINE, half + (outer + 1) * FINE), slice(lane, lane + LANE)),
                    s,
                )
    for j in range(groups):
        for a in range(fold):
            c, s = product_rows(f2_ref, a, slice(j * LANE, (j + 1) * LANE), band_rows)
            put_turn(f2_buf.at[j], a * band_rows, band_rows, 0, LANE, LANE, LANE, c, s)

    for pair in range(groups // 2):
        for a in range(2):
            for side in range(2):
                j = 2 * pair + side
                for first in range(0, half, FINE):
                    value = packed_ref[j, pl.ds(2 * first + a, FINE, stride=2), :]
                    put(
                        x_buf.at[pair % x_buf.shape[0], a],
                        (slice(first, first + FINE), slice(side * LANE, (side + 1) * LANE)),
                        value,
                    )
        even = split_dot(f1_buf.at[0], x_buf.at[pair % x_buf.shape[0], 0], NN)
        odd = split_dot(f1_buf.at[1], x_buf.at[pair % x_buf.shape[0], 1], NN)
        for block in range(half // FINE):
            rows = slice(block * FINE, (block + 1) * FINE)
            lower = slice(half + block * FINE, half + (block + 1) * FINE)
            for side in range(2):
                j = 2 * pair + side
                lanes = slice(side * LANE, (side + 1) * LANE)
                for r in range(2):
                    c, s = product_rows(
                        twist1_ref, r * (half // FINE) + block, slice(j * LANE, (j + 1) * LANE)
                    )
                    if r:
                        a, b = even[rows, lanes] - odd[rows, lanes], even[lower, lanes] - odd[lower, lanes]
                    else:
                        a, b = even[rows, lanes] + odd[rows, lanes], even[lower, lanes] + odd[lower, lanes]
                    target = slice(r * half + block * FINE, r * half + (block + 1) * FINE)
                    put(y_buf.at[j % y_buf.shape[0]], (target, slice(0, LANE)), a * c - b * s)
                    put(y_buf.at[j % y_buf.shape[0]], (target, slice(LANE, 2 * LANE)), a * s + b * c)
        for side in range(2):
            j = 2 * pair + side
            part_ref[j] = split_dot(f2_buf.at[j], y_buf.at[j % y_buf.shape[0]], NT)

    for q in range(inner // LANE):
        for band in range(bands):
            for j in range(groups):
                source = segment_rows + (q * bands + band) * member_rows
                target = (band * groups + j) * member_rows
                weight_ref[q, target : target + member_rows, :] = packed_ref[
                    j, source : source + member_rows, :
                ]

    for a in range(fold):
        @pl.loop(0, 1)
        def _(_):
            zero = jnp.zeros((LANE - reach, inner), BF16)
            for m in range(templates):
                for slot in range(2):
                    c_buf[m, a, slot, reach:LANE, :] = zero
                    c_buf[m, a, slot, LANE + reach :, :] = zero

    total = jnp.zeros((8, LANE), F32)
    for a in range(fold):
        for q0 in range(0, band_rows, COARSE):
            rows = slice(a * band_rows + q0, a * band_rows + q0 + COARSE)
            lower = slice(LANE + a * band_rows + q0, LANE + a * band_rows + q0 + COARSE)
            for lane in range(0, inner, LANE):
                lanes = slice(lane, lane + LANE)
                values = [
                    (part_ref[j, rows, lanes], part_ref[j, lower, lanes]) for j in range(groups)
                ]
                sums = small_dft(values, -1, list(range(bands)))
                for band in range(bands):
                    b = band * band_rows + q0
                    amp = amp_ref[a * reach + b : a * reach + b + COARSE, lanes]
                    density = weight_ref[lane // LANE, pl.ds(a + fold * b, COARSE, stride=fold), :]
                    weight = amp * density
                    power = weight * amp
                    total = total + power[:8] + power[8:]
                    weight = weight * scale
                    x_re = sums[band][0] * weight
                    x_im = sums[band][1] * weight
                    for m in range(templates):
                        cs, ss = [], []
                        for n in range(b // 8, b // 8 + COARSE // 8):
                            c1 = chirp_ref[m, 0, n : n + 1, lanes]
                            s1 = chirp_ref[m, 1, n : n + 1, lanes]
                            near = slice(COARSE + 8 * a, COARSE + 8 * (a + 1))
                            c0 = chirp_ref[m, 0, near, lanes]
                            s0 = chirp_ref[m, 1, near, lanes]
                            cs.append(c1 * c0 - s1 * s0)
                            ss.append(s1 * c0 + c1 * s0)
                        c = jnp.concatenate(cs, axis=0)
                        s = jnp.concatenate(ss, axis=0)
                        put(c_buf.at[m, a], (slice(b, b + COARSE), lanes), x_re * c - x_im * s)
                        put(
                            c_buf.at[m, a],
                            (slice(LANE + b, LANE + b + COARSE), lanes),
                            x_re * s + x_im * c,
                        )
    total = jnp.sum(jnp.sum(total, axis=0, keepdims=True), axis=1, keepdims=True)
    norm = 1.0 / jnp.sqrt(total)

    height = i2_buf.shape[2] // 2
    steps = half // LANE
    for rho in range(2):
        for outer in range(height // FINE):
            c, s = product_rows(i2_ref, rho * (height // FINE) + outer)
            put_turn(i2_buf.at[rho], outer * FINE, FINE, 0, half, height, half, c, s)

    per_step = LANE // FINE
    row_stride = 2 * templates * fold * steps

    @pl.loop(0, steps)
    def _(h):
        for a in range(fold):
            for o in range(per_step):
                c, s = product_rows(i1_ref, h * per_step + o, slice(a * LANE, (a + 1) * LANE))
                put_turn(i1_buf.at[a], o * FINE, FINE, 0, LANE, LANE, LANE, c, s)
        mixed = [
            [split_dot(i1_buf.at[a], c_buf.at[m, a], NN) for a in range(fold)]
            for m in range(templates)
        ]
        for o in range(per_step):
            rows = slice(o * FINE, (o + 1) * FINE)
            lower = slice(LANE + o * FINE, LANE + (o + 1) * FINE)
            for lane in range(0, half, LANE):
                sides = []
                for first in (lane, half + lane):
                    lanes = slice(first, first + LANE)
                    turns = [
                        product_rows(twist2_ref, (r * steps + h) * per_step + o, lanes)
                        for r in range(fold)
                    ]
                    both = []
                    for m in range(templates):
                        values = [(mixed[m][a][rows, lanes], mixed[m][a][lower, lanes]) for a in range(fold)]
                        outs = small_dft(values, 1, list(range(fold)))
                        both.append(
                            [
                                (a * c - b * s, a * s + b * c)
                                for (a, b), (c, s) in ((outs[r], turns[r]) for r in range(fold))
                            ]
                        )
                    sides.append(both)
                for m in range(templates):
                    for r in range(fold):
                        target = slice(r * LANE + o * FINE, r * LANE + (o + 1) * FINE)
                        for part in range(2):
                            near, far = sides[0][m][r][part], sides[1][m][r][part]
                            lanes = slice(part * half + lane, part * half + lane + LANE)
                            put(g_buf.at[m, 0], (target, lanes), near + far)
                            put(g_buf.at[m, 1], (target, lanes), near - far)
        for m in range(templates):
            for rho in range(2):
                z = split_dot(i2_buf.at[rho], g_buf.at[m, rho], NT)
                z_re, z_im = z[:height], z[height:]
                size = jnp.sqrt(z_re * z_re + z_im * z_im) * norm
                for r in range(fold):
                    first = ((rho * fold + r) * steps + h) * templates + m
                    out_ref[pl.ds(first, height, stride=row_stride), :] = size[:, r * LANE : (r + 1) * LANE]


def local(strain, psd_bins, psd_values, chirp_slope, chirp_curve):
    groups = lax.axis_size("tmpl")
    own_part = strain[0]
    half_len = own_part.shape[0]
    sub_len = 2 * half_len
    total_len = sub_len * groups
    inner = sub_len // LANE
    outer = total_len // inner
    depth = 3 * outer // 8
    k_low = total_len // 200
    k_cut = 3 * total_len // 8
    bands = 3 * groups // 8
    templates = chirp_slope.shape[0]
    member_len = psd_bins.shape[1]
    member_rows = member_len // inner
    fold = outer // (2 * LANE)
    reach = depth // fold
    assert (fold * inner) ** 2 % total_len == 0 and 2 * fold * inner**2 % total_len == 0
    assert total_len & (total_len - 1) == 0 and reach <= 8 * COARSE and reach <= LANE

    extra = bands * member_len // LANE
    table_shapes = [
        jax.ShapeDtypeStruct((templates, 2, COARSE + 8 * fold, inner), F32),
        jax.ShapeDtypeStruct((depth, inner), F32),
    ]
    vmem = pl.BlockSpec(memory_space=pltpu.VMEM)
    smem = pl.BlockSpec(memory_space=pltpu.SMEM)
    own_rows = own_part.reshape(-1, LANE)
    rows = 2 * own_rows.shape[0] + extra
    if groups == 8:
        packed, chirp, amplitude = pl.pallas_call(
            functools.partial(gather_kernel, bands, inner, total_len),
            in_specs=[vmem, vmem, vmem, smem, smem],
            out_specs=[vmem, vmem, vmem],
            out_shape=[jax.ShapeDtypeStruct((groups, rows, LANE), F32)] + table_shapes,
            scratch_shapes=[
                pltpu.VMEM((extra, LANE), jnp.int32),
                pltpu.SemaphoreType.DMA((3, 9)),
                pltpu.SemaphoreType.DMA((3, 9)),
                pltpu.SemaphoreType.DMA((5,)),
                pltpu.SemaphoreType.DMA((5,)),
            ],
            compiler_params=pltpu.CompilerParams(collective_id=0, has_side_effects=True),
            name="gather",
        )(own_rows, psd_bins, psd_values, chirp_slope, chirp_curve)
    else:
        tail = shifted(own_part, "tm", 1).reshape(-1, LANE)
        inv_psd = pl.pallas_call(
            functools.partial(density_kernel, bands, inner),
            out_shape=jax.ShapeDtypeStruct((extra, LANE), F32),
            scratch_shapes=[pltpu.VMEM((extra, LANE), jnp.int32)],
            name="density",
        )(psd_bins, psd_values)
        packed = lax.all_gather(
            jnp.concatenate([tail, own_rows, inv_psd], axis=0), "tmpl", axis=0, tiled=False
        )
        chirp, amplitude = pl.pallas_call(
            functools.partial(table_kernel, total_len),
            in_specs=[smem, smem],
            out_shape=table_shapes,
            name="tables",
        )(chirp_slope, chirp_curve)

    half = inner // 2
    place = np.arange(outer)
    sample = (place % LANE) * groups + place // LANE
    step = np.arange(half)
    band_rows = LANE // fold
    f1 = base_table(half, np.concatenate([2 * step, 2 * step + 1]), inner, -1.0)
    twist1 = base_table(inner, sample, total_len, -1.0)
    f2 = factor_table(np.arange(fold), fold * np.arange(band_rows), sample, outer, -1.0)
    member = np.arange(fold)[:, None] + fold * np.arange(LANE)[None, :]
    i1 = base_table(2 * LANE, member.reshape(-1), outer, 1.0)
    twist2 = base_table(outer, np.arange(inner), total_len, 1.0)
    late = half + np.arange(2)[:, None] + 2 * FINE * np.arange(half // 2 // FINE)[None, :]
    i2 = factor_table(late.reshape(-1), 2 * np.arange(FINE), step, inner, 1.0)

    out_rows = half * (outer // LANE) * templates
    flat = pl.pallas_call(
        functools.partial(
            filter_kernel, inner, member_rows, bands, templates, 1.0 / math.sqrt(total_len)
        ),
        in_specs=[vmem] * 9,
        out_specs=vmem,
        out_shape=jax.ShapeDtypeStruct((out_rows, LANE), F32),
        scratch_shapes=[
            pltpu.VMEM((2, 2, inner, half), BF16),
            pltpu.VMEM((2, 2, 2, half, 2 * LANE), BF16),
            pltpu.VMEM((groups, 2, 2 * LANE, 2 * LANE), BF16),
            pltpu.VMEM((4, 2, inner, 2 * LANE), BF16),
            pltpu.VMEM((groups, 2 * LANE, inner), F32),
            pltpu.VMEM((inner // LANE, depth, LANE), F32),
            pltpu.VMEM((templates, fold, 2, 2 * LANE, inner), BF16),
            pltpu.VMEM((fold, 2, 2 * LANE, 2 * LANE), BF16),
            pltpu.VMEM((2, 2, half, inner), BF16),
            pltpu.VMEM((templates, 2, 2, fold * LANE, inner), BF16),
        ],
        compiler_params=pltpu.CompilerParams(vmem_limit_bytes=VMEM_LIMIT),
        name="filter",
    )(packed, amplitude, chirp, f1, twist1, f2, i1, twist2, i2)
    result = flat.reshape(-1, templates, LANE)
    return jnp.transpose(result, (1, 0, 2)).reshape(templates, -1)


def solution(mesh):
    placed = (P("tmpl", "tm"), P(None, "tmpl"), P("tm", None), P("tmpl"), P("tmpl"))
    return jax.shard_map(
        local, mesh=mesh, in_specs=placed, out_specs=P("tmpl", "tm"), check_vma=False
    )
```
